32 devices in a mesh: groups: 2 (over y), seq: 4 (over z), section: 2 (over x), kv: 2 (over core).
Axes of the slice: x: 2, y: 2, z: 4, core: 2. Of those that a mesh axis runs over, the one named last changes fastest.
Arguments:
- queries: bfloat16 [4, 1024, 2560], P(('groups', 'section'), 'seq', 'kv'), parts along dimension 0, may hold values from -128 to 128
- key_rows: bfloat16 [4, 1024, 512], P(('groups', 'section'), 'seq', 'kv'), parts along dimension 0, may hold values from -4 to 4
- values: bfloat16 [4, 1024, 512], P(('groups', 'section'), 'seq', 'kv'), parts along dimension 0, may hold values from -6 to 6
- lengths: int32 [4, 3], P(('groups', 'section')), parts along dimension 0, may hold values from 1 to 32, 64 in all within a row
- block_order: int32 [4, 4], P(('groups', 'section')), parts along dimension 0, may hold values from 0 to 3, each once within a row
- page_owner: int32 [4, 64, 1], P(('groups', 'section')), parts along dimension 0, may hold values from 0 to 3; in each aligned block of 16 rows (0 to 15, 16 to 31, ..., all dimensions but the last counted through in order) at most 8 rows name the same one
Outputs:
- handed: bfloat16 [4, 1024, 2560], P(('groups', 'section'), 'seq', 'kv'), parts along dimension 0
- cache_keys: bfloat16 [4, 4, 512, 512], P(('groups', 'section'), 'seq', None, 'kv'), parts along dimension 0
- cache_values: bfloat16 [4, 4, 512, 512], P(('groups', 'section'), 'seq', None, 'kv'), parts along dimension 0
The draws below stay inside these ranges and needn't reach their ends.
There are 2 independent parts, one for each index of `groups`. The reference program is written for one: setup_inputs(seed, part) draws one part's arguments, and reference() takes and returns one part's arrays. A program takes and returns all parts, laid end to end along the dimension named above; each array names one. Nothing has to cross between parts.
Inputs may be any that keep to these rules, and one draw needn't show every extreme that they name: `lengths`: lengths sum to 64; the longest request has exactly 32 pages. `block_order`: each row is a permutation of the seq indices. `page_owner`: among the 16 pages of one aligned device block, no owner is named more than 8 times.
All inputs are finite; a program needn't handle non-finite values.
Results may differ from the reference program's by a relative error of at most 0.0038.
Values may be sent and summed in bfloat16 or wider, within the bound.
No kernel may reach another device: no remote copies, remote signals or barrier semaphores. Data moves between devices by JAX's collectives and lax.ppermute only.
A program may use at most 64 MiB of HBM per device.

```python
import math
import jax
import jax.numpy as jnp
import numpy as np
from jax import lax

QUERY_HEADS = 20
LOCAL_KV_HEADS = 4
HEAD_SIZE = 128
PAGE_TOKENS = 16
REQS = 3
TOK_DEV = 256
RELAY_SECTIONS = 2
SECTION_TOKENS = 1024
PAGES = 64
DEVICE_PAGES = 16
MOST_PAGES = 32
SOURCE_SLOTS = 8
OWNER_CACHE_ROWS = 512
N_SEQ = 4


def shared_pair(base_key):
    initial_random_key = jax.random.fold_in(base_key, 7101)
    second_key = jax.random.fold_in(base_key, 7102)
    per_head_keys = jnp.clip(jax.random.normal(initial_random_key, (RELAY_SECTIONS, SECTION_TOKENS, LOCAL_KV_HEADS, HEAD_SIZE), jnp.float32), -4.0, 4.0)
    per_head_queries = jnp.clip(jax.random.normal(second_key, (RELAY_SECTIONS, SECTION_TOKENS, QUERY_HEADS, HEAD_SIZE), jnp.float32), -4.0, 4.0)
    return (per_head_queries.reshape(RELAY_SECTIONS, SECTION_TOKENS, QUERY_HEADS * HEAD_SIZE), per_head_keys.reshape(RELAY_SECTIONS, SECTION_TOKENS, LOCAL_KV_HEADS * HEAD_SIZE))


def draw_queries(key, part):
    return shared_pair(key)[0].astype(jnp.bfloat16)


def draw_key_rows(key, part):
    return shared_pair(key)[1].astype(jnp.bfloat16)


def block_levels(stream_key, shape, shards, least, largest):
    def one(dim, blocks):
        steps = jax.random.uniform(jax.random.fold_in(jax.random.fold_in(stream_key, 6), dim), (blocks,), jnp.float32, least / len(shards), largest / len(shards))
        return jnp.repeat(jnp.exp(steps), shape[dim] // blocks).reshape((-1,) + (1,) * (len(shape) - dim - 1))

    factor_of = one(*shards[0])
    for cut in shards[1:]:
        factor_of = factor_of * one(*cut)
    return factor_of


def split_up(amount, total, limit, lean):
    weights = [(1 << 20) // math.isqrt(standing ** lean) + 1 for standing in range(2, amount + 1)]
    surplus, holding = total - limit - (amount - 1), [1] * (amount - 1)
    while surplus > 0:
        movable = [i for i in range(amount - 1) if holding[i] < limit]
        mass, budget = sum([weights[i] for i in movable]), surplus
        for i in movable:
            more = min(limit - holding[i], max(1, budget * weights[i] // mass), surplus)
            holding[i] = holding[i] + more
            surplus = surplus - more
    return np.array([limit] + holding)


def ragged_sizes(key, number_of, total, limit, skew):
    if number_of == 2:
        one = jax.random.randint(key, (), max(1, total - limit), min(limit, total - 1) + 1)
        return jnp.stack([one, total - one])
    tallies = jnp.asarray(split_up(number_of, total, limit, skew), jnp.int32)
    pairs = (number_of - 1) // 2
    source_of, receiver = tallies[1:1 + 2 * pairs:2], tallies[2:2 + 2 * pairs:2]
    margin = jnp.minimum(source_of - 1, limit - receiver)
    passed = jax.random.randint(jax.random.fold_in(key, 1), (pairs,), 0, 1 << 20) % (margin + 1)
    tallies = tallies.at[1:1 + 2 * pairs:2].set(source_of - passed).at[2:2 + 2 * pairs:2].set(receiver + passed)
    return tallies[jax.random.permutation(jax.random.fold_in(key, 2), number_of)]


def shared_out(rng, own, number, rows, count, top, most, skew):
    order = jax.random.permutation(rng, count)
    packed, usual = load_shares(count, rows * top, most, skew, True), load_shares(count, rows * top, most, skew, False)
    places = jnp.arange(count)

    def named(sizes, offset_by):
        used = int((sizes > 0).sum())
        fixed = max(1, used // 4)
        moved = fixed + (places - fixed + offset_by * (used - fixed)) % max(1, count - fixed)
        return jnp.zeros((count,), jnp.int32).at[order[jnp.where(places < fixed, places, moved)]].set(jnp.asarray(sizes, jnp.int32))

    sizes = jnp.where(number % 4 == 0, named(packed, number // 4), named(usual, number - number // 4 - 1))
    mixed = jax.random.permutation(jax.random.fold_in(own, 3), count)
    source_of, taker = mixed[0:count // 2 * 2:2], mixed[1:count // 2 * 2:2]
    margin = jnp.minimum(sizes[source_of] - 1, most - sizes[taker]) // 2
    margin = jnp.where((source_of == order[0]) | (taker == order[0]) | (sizes[taker] == 0), 0, jnp.maximum(margin, 0))
    moved = jax.random.randint(jax.random.fold_in(own, 4), (count // 2,), 0, 1 << 20) % (margin + 1)
    sizes = sizes.at[source_of].add(-moved).at[taker].add(moved)
    labels = jnp.searchsorted(jnp.cumsum(sizes), jnp.arange(rows * top), side="right").astype(jnp.int32)
    listing = labels.reshape(top, rows).T
    listing = listing[jax.random.permutation(jax.random.fold_in(own, 1), rows)]
    offset_by = jax.random.randint(jax.random.fold_in(own, 2), (rows, 1), 0, top)
    return jnp.take_along_axis(listing, (jnp.arange(top)[None, :] + offset_by) % top, axis=1)


def load_shares(number_of, total, limit, skew, full):
    loads = [(1 << 20) // math.isqrt(rank ** skew) + 1 for rank in range(1, number_of + 1)]
    largest = limit if full else min(limit, max(-(-total // number_of), total * loads[0] // sum(loads)))
    least = 1 if total - largest >= number_of - 1 else 0
    given, spare = [largest] + [least] * (number_of - 1), total - largest - least * (number_of - 1)
    while spare > 0:
        free = [i for i in range(1, number_of) if given[i] < largest] or [i for i in range(1, number_of) if given[i] < limit]
        mass, budget = sum([loads[i] for i in free]), spare
        for i in free:
            addition = min(limit - given[i], max(1, budget * loads[i] // mass), spare)
            given[i] = given[i] + addition
            spare = spare - addition
    return np.array(given)


def normal_values(stream_key, shape, width, most, cuts=(), kind=jnp.bfloat16):
    level = block_levels(stream_key, shape, cuts, -0.22, 0.18) if cuts else 1.0
    array = jax.random.normal(stream_key, shape, jnp.float32) * width * level
    return jnp.minimum(jnp.maximum(array, -most), most).astype(kind)


def setup_inputs(seed: int = 0, part: int = 0) -> dict:
    key_list = jax.random.split(jax.random.key(seed), 7)
    own_keys = jax.random.split(jax.random.fold_in(key_list[6], part), 7)
    queries = draw_queries(jax.random.fold_in(jax.random.fold_in(key_list[6], part), 71), part)
    key_rows = draw_key_rows(jax.random.fold_in(jax.random.fold_in(key_list[6], part), 71), part)
    values = normal_values(own_keys[2], (RELAY_SECTIONS, SECTION_TOKENS, LOCAL_KV_HEADS * HEAD_SIZE), 1.0, 6.0, ((0, 2), (1, 4), (2, 2)))
    lengths = jax.vmap(lambda own: ragged_sizes(own, REQS, PAGES, MOST_PAGES, 2))(jax.random.split(own_keys[3], RELAY_SECTIONS)).reshape((RELAY_SECTIONS, REQS)).astype(jnp.int32)
    block_order = jax.vmap(lambda own: jax.random.permutation(own, N_SEQ))(jax.random.split(own_keys[4], RELAY_SECTIONS)).reshape((RELAY_SECTIONS, N_SEQ)).astype(jnp.int32)
    page_owner_keys = jax.random.split(jax.random.fold_in(own_keys[5], 1), RELAY_SECTIONS * PAGES // DEVICE_PAGES)
    page_owner_turns = jax.random.permutation(jax.random.fold_in(own_keys[5], 3), RELAY_SECTIONS * PAGES // DEVICE_PAGES)
    page_owner = jax.vmap(lambda own, number: shared_out(jax.random.fold_in(own_keys[5], 2), own, number, DEVICE_PAGES, N_SEQ, 1, SOURCE_SLOTS, 2))(page_owner_keys, page_owner_turns).reshape((RELAY_SECTIONS, PAGES, 1))
    return dict(queries=queries, key_rows=key_rows, values=values, lengths=lengths, block_order=block_order, page_owner=page_owner)


def reference(queries, key_rows, values, lengths, block_order, page_owner):
    query_group_width = QUERY_HEADS // LOCAL_KV_HEADS
    query_tile_rows = math.gcd(SECTION_TOKENS, 512)
    block_count = SECTION_TOKENS // query_tile_rows
    inv_root = 1.0 / math.sqrt(HEAD_SIZE)
    row_index = jnp.arange(SECTION_TOKENS, dtype=jnp.int32)

    def attention_section(inputs):
        section_queries, relay_key_rows, relay_value_rows, section_lengths, section_blocks = inputs
        starts = jnp.cumsum(section_lengths) - section_lengths
        position = (section_blocks[row_index // TOK_DEV] * TOK_DEV + row_index % TOK_DEV).astype(jnp.int32)
        request = lax.optimization_barrier(jnp.sum((position[:, None] // PAGE_TOKENS >= starts[None, :]).astype(jnp.int32), axis=1)) - 1
        per_head_keys = relay_key_rows.astype(jnp.float32).reshape(SECTION_TOKENS, LOCAL_KV_HEADS, HEAD_SIZE)
        per_head_values = relay_value_rows.astype(jnp.float32).reshape(SECTION_TOKENS, LOCAL_KV_HEADS, HEAD_SIZE)

        def query_part(items):
            slice_query_rows, part_pos, part_req = items
            head_split = slice_query_rows.astype(jnp.float32).reshape(query_tile_rows, LOCAL_KV_HEADS, query_group_width, HEAD_SIZE)
            scores = jnp.einsum('qgjd,kgd->qgjk', head_split, per_head_keys, precision=lax.Precision.HIGHEST) * inv_root
            allowed = ((request[None, :] == part_req[:, None]) & (position[None, :] <= part_pos[:, None]))[:, None, None, :]
            scores = jnp.where(allowed, scores, -1e+30)
            highest = lax.optimization_barrier(jnp.max(scores, axis=-1, keepdims=True))
            weights = jnp.where(allowed, jnp.exp(scores - highest), 0.0)
            total = lax.optimization_barrier(jnp.sum(weights, axis=-1))
            rounded = lax.optimization_barrier(weights.astype(jnp.bfloat16)).astype(jnp.float32)
            mixed = jnp.einsum('qgjk,kgd->qgjd', rounded, per_head_values, precision=lax.Precision.HIGHEST) / total[..., None]
            return mixed.reshape(query_tile_rows, QUERY_HEADS * HEAD_SIZE).astype(jnp.bfloat16)
        pieces = lax.map(query_part, (section_queries.reshape(block_count, query_tile_rows, QUERY_HEADS * HEAD_SIZE), position.reshape(block_count, query_tile_rows), request.reshape(block_count, query_tile_rows)))
        return pieces.reshape(SECTION_TOKENS, QUERY_HEADS * HEAD_SIZE)
    context = lax.map(attention_section, (queries, key_rows, values, lengths, block_order))
    handed = jnp.roll(context, 1, axis=0)

    def cache_section(inputs):
        relay_key_rows, relay_value_rows, section_blocks, section_owner = inputs
        owners = section_owner[:, 0].reshape(N_SEQ, DEVICE_PAGES)[section_blocks]
        page_index = jnp.arange(DEVICE_PAGES, dtype=jnp.int32)
        earlier = (owners[:, None, :] == owners[:, :, None]) & (page_index[None, :] < page_index[:, None])[None]
        slot_rank = lax.optimization_barrier(jnp.sum(earlier.astype(jnp.int32), axis=2))
        sources = jnp.arange(N_SEQ, dtype=jnp.int32)[:, None]
        destination_slot = (owners * (N_SEQ * SOURCE_SLOTS) + sources * SOURCE_SLOTS + slot_rank).reshape(-1).astype(jnp.int32)
        paged_key_cache = relay_key_rows.reshape(N_SEQ * DEVICE_PAGES, PAGE_TOKENS * LOCAL_KV_HEADS * HEAD_SIZE)
        paged_value_cache = relay_value_rows.reshape(N_SEQ * DEVICE_PAGES, PAGE_TOKENS * LOCAL_KV_HEADS * HEAD_SIZE)
        blank_pages = jnp.zeros((N_SEQ * N_SEQ * SOURCE_SLOTS, PAGE_TOKENS * LOCAL_KV_HEADS * HEAD_SIZE), jnp.bfloat16)
        cache_key_rows = blank_pages.at[destination_slot].set(paged_key_cache).reshape(N_SEQ, OWNER_CACHE_ROWS, LOCAL_KV_HEADS * HEAD_SIZE)
        cache_value_rows = blank_pages.at[destination_slot].set(paged_value_cache).reshape(N_SEQ, OWNER_CACHE_ROWS, LOCAL_KV_HEADS * HEAD_SIZE)
        return (cache_key_rows, cache_value_rows)
    cache_keys, cache_values = lax.map(cache_section, (key_rows, values, block_order, page_owner))
    return (handed, cache_keys, cache_values)
```

```python
import math

import jax
import jax.numpy as jnp
from jax import lax
from jax.experimental import pallas as pl
from jax.experimental.pallas import tpu as pltpu
from jax.sharding import PartitionSpec as P

HEAD_SIZE = 128
MASKED = -1e30
EXP2_SCALE = math.log2(math.e) / math.sqrt(HEAD_SIZE)


SMEM = pl.BlockSpec(memory_space=pltpu.SMEM)
VMEM = pl.BlockSpec(memory_space=pltpu.VMEM)


def partner(index, turn, count):
    if count & (count - 1) == 0:
        return index ^ turn
    return (index + turn) % count


def source_of(index, turn, count):
    if count & (count - 1) == 0:
        return jnp.bitwise_xor(index, turn)
    return lax.rem(index - turn + count, count)


def split_heads_kernel(keys_ref, values_ref, *message_refs):
    rows = keys_ref.shape[1]
    for head, message_ref in enumerate(message_refs):
        columns = pl.ds(head * HEAD_SIZE, HEAD_SIZE)
        message_ref[:rows, :] = keys_ref[0, :, columns]
        message_ref[rows:, :] = values_ref[0, :, columns]


def split_heads(key_rows, values):
    rows, width = key_rows.shape[1:]
    message = jax.ShapeDtypeStruct((2 * rows, HEAD_SIZE), key_rows.dtype)
    return pl.pallas_call(
        split_heads_kernel,
        out_shape=[message] * (width // HEAD_SIZE),
        in_specs=[VMEM] * 2,
        out_specs=[VMEM] * (width // HEAD_SIZE),
        name="split_heads",
    )(key_rows, values)


def gather_turns(message):
    count = lax.axis_size("seq")
    received = [message]
    for turn in range(1, count):
        route = [(i, partner(i, turn, count)) for i in range(count)]
        received.append(lax.ppermute(message, "seq", route))
    return received


def attend_kernel(lengths_ref, order_ref, queries_ref, *refs, count, page_tokens):
    block_refs = refs[:count]
    context_ref = refs[count]
    bias_ref, max_ref, sum_ref, acc_ref = refs[count + 1 :]
    rows = queries_ref.shape[1]
    heads = queries_ref.shape[2] // HEAD_SIZE
    own = lax.axis_index("seq")
    own_block = order_ref[0, own]
    pages = rows // page_tokens

    row_page = own_block * pages + lax.broadcasted_iota(jnp.int32, (rows, rows), 0) // page_tokens
    first_page = own_block * pages
    row_start = jnp.zeros((rows, rows), jnp.int32)
    first_start = jnp.int32(0)
    start = jnp.int32(0)
    for request in range(lengths_ref.shape[1]):
        row_start = jnp.where(row_page >= start, start, row_start)
        first_start = jnp.where(first_page >= start, start, first_start)
        start = start + lengths_ref[0, request]
    row_start = row_start * page_tokens
    column = lax.broadcasted_iota(jnp.int32, (rows, rows), 1)

    def scores_of(head, block_ref):
        query = queries_ref[0, :, head * HEAD_SIZE : (head + 1) * HEAD_SIZE]
        return (
            lax.dot_general(
                query,
                block_ref[:rows, :],
                (((1,), (1,)), ((), ())),
                preferred_element_type=jnp.float32,
            )
            + bias_ref[...]
        )

    def weighted(weight, block_ref):
        return jnp.dot(
            weight.astype(jnp.bfloat16), block_ref[rows:, :], preferred_element_type=jnp.float32
        )

    def folded(weight):
        total = weight[:, :HEAD_SIZE]
        for piece in range(1, weight.shape[1] // HEAD_SIZE):
            total = total + weight[:, piece * HEAD_SIZE : (piece + 1) * HEAD_SIZE]
        return total

    row = lax.broadcasted_iota(jnp.int32, (rows, rows), 0)
    allowed = (own_block * rows + column >= row_start) & (column <= row)
    bias_ref[...] = jnp.where(allowed, 0.0, MASKED)
    for head in range(heads):
        scores = scores_of(head, block_refs[0])
        top = jnp.max(scores, axis=1, keepdims=True)
        weight = jnp.exp2((scores - top) * EXP2_SCALE)
        max_ref[head] = jnp.broadcast_to(top, (rows, HEAD_SIZE))
        sum_ref[head] = folded(weight)
        acc_ref[head] = weighted(weight, block_refs[0])

    for turn in range(1, count):
        block_ref = block_refs[turn]
        block = order_ref[0, source_of(own, turn, count)]
        needed = (block < own_block) & ((block + 1) * pages > first_start)

        @pl.when(needed)
        def _():
            bias_ref[...] = jnp.where(block * rows + column >= row_start, 0.0, MASKED)
            for head in range(heads):
                scores = scores_of(head, block_ref)
                before = max_ref[head]
                top = jnp.maximum(before, jnp.max(scores, axis=1, keepdims=True))
                rescale = jnp.exp2((before - top) * EXP2_SCALE)
                weight = jnp.exp2((scores - top[:, :1]) * EXP2_SCALE)
                max_ref[head] = top
                sum_ref[head] = sum_ref[head] * rescale + folded(weight)
                acc_ref[head] = acc_ref[head] * rescale + weighted(weight, block_ref)

    for head in range(heads):
        total = jnp.sum(sum_ref[head], axis=1, keepdims=True)
        context_ref[0, :, head * HEAD_SIZE : (head + 1) * HEAD_SIZE] = (
            acc_ref[head] / total
        ).astype(context_ref.dtype)


def attend(lengths, block_order, queries, blocks, head, kv_heads, page_tokens):
    rows, width = queries.shape[1:]
    count = len(blocks)
    width = width // kv_heads
    group = width // HEAD_SIZE
    pairs = group * rows * rows * (count + 1) // 2

    def kernel(*refs):
        attend_kernel(*refs, count=count, page_tokens=page_tokens)

    return pl.pallas_call(
        kernel,
        grid=(1,),
        out_shape=jax.ShapeDtypeStruct((1, rows, width), queries.dtype),
        in_specs=[
            SMEM,
            SMEM,
            pl.BlockSpec((1, rows, width), lambda i: (0, 0, head)),
        ]
        + [pl.BlockSpec((2 * rows, HEAD_SIZE), lambda i: (0, 0)) for _ in blocks],
        out_specs=pl.BlockSpec((1, rows, width), lambda i: (0, 0, 0)),
        scratch_shapes=[
            pltpu.VMEM((rows, rows), jnp.float32),
            pltpu.VMEM((group, rows, HEAD_SIZE), jnp.float32),
            pltpu.VMEM((group, rows, HEAD_SIZE), jnp.float32),
            pltpu.VMEM((group, rows, HEAD_SIZE), jnp.float32),
        ],
        cost_estimate=pl.CostEstimate(
            flops=4 * pairs * HEAD_SIZE,
            bytes_accessed=2 * 2 * rows * width + count * 4 * rows * HEAD_SIZE,
            transcendentals=pairs,
        ),
        name="attend",
    )(lengths, block_order, queries, *blocks)


def cache_kernel(order_ref, owner_ref, *refs, count, kv_heads, page_tokens, slots):
    block_refs = refs[: count * kv_heads]
    keys_ref, values_ref = refs[count * kv_heads :]
    rows = block_refs[0].shape[0] // 2
    pages = rows // page_tokens
    own = lax.axis_index("seq")
    keys_ref[...] = jnp.zeros_like(keys_ref)
    values_ref[...] = jnp.zeros_like(values_ref)
    for turn in range(count):
        source = source_of(own, turn, count)
        block = order_ref[0, source]

        def page_step(page, rank):
            mine = owner_ref[block * pages + page] == own

            @pl.when(mine)
            def _():
                take = pl.ds(pl.multiple_of(page * page_tokens, page_tokens), page_tokens)
                take_value = pl.ds(
                    pl.multiple_of(rows + page * page_tokens, page_tokens), page_tokens
                )
                put = pl.ds(
                    pl.multiple_of((source * slots + rank) * page_tokens, page_tokens), page_tokens
                )
                for head in range(kv_heads):
                    columns = pl.ds(head * HEAD_SIZE, HEAD_SIZE)
                    block_ref = block_refs[turn * kv_heads + head]
                    keys_ref[0, 0, put, columns] = block_ref[take, :]
                    values_ref[0, 0, put, columns] = block_ref[take_value, :]

            return rank + mine.astype(jnp.int32)

        lax.fori_loop(0, pages, page_step, jnp.int32(0))


def build_cache(block_order, owners, blocks, kv_heads, page_tokens, slots):
    count = len(blocks) // kv_heads
    cache = jax.ShapeDtypeStruct(
        (1, 1, count * slots * page_tokens, kv_heads * HEAD_SIZE), blocks[0].dtype
    )

    def kernel(*refs):
        cache_kernel(
            *refs, count=count, kv_heads=kv_heads, page_tokens=page_tokens, slots=slots
        )

    return pl.pallas_call(
        kernel,
        out_shape=[cache, cache],
        in_specs=[SMEM, SMEM] + [VMEM] * len(blocks),
        out_specs=[VMEM, VMEM],
        name="build_cache",
    )(block_order, owners, *blocks)


def body(queries, key_rows, values, lengths, block_order, page_owner):
    count = lax.axis_size("seq")
    sections = lax.axis_size("section")
    rows = key_rows.shape[1]
    kv_heads = key_rows.shape[2] // HEAD_SIZE
    device_pages = page_owner.shape[1] // count
    page_tokens = rows // device_pages
    slots = max(2, 2 * device_pages // count)
    owners = page_owner.reshape(page_owner.shape[1])

    messages = split_heads(key_rows, values)
    gathered = [gather_turns(message) for message in messages]
    onward = [(i, (i + 1) % sections) for i in range(sections)]
    handed = []
    for head in range(kv_heads):
        context = attend(
            lengths, block_order, queries, gathered[head], head, kv_heads, page_tokens
        )
        handed.append(lax.ppermute(context, "section", onward))
    blocks = [gathered[head][turn] for turn in range(count) for head in range(kv_heads)]
    cache_keys, cache_values = build_cache(
        block_order, owners, blocks, kv_heads, page_tokens, slots
    )
    return (jnp.concatenate(handed, axis=2), cache_keys, cache_values)


def solution(mesh):
    in_specs = (
        P(("groups", "section"), "seq", "kv"),
        P(("groups", "section"), "seq", "kv"),
        P(("groups", "section"), "seq", "kv"),
        P(("groups", "section"), None),
        P(("groups", "section"), None),
        P(("groups", "section"), None, None),
    )
    out_specs = (
        P(("groups", "section"), "seq", "kv"),
        P(("groups", "section"), "seq", None, "kv"),
        P(("groups", "section"), "seq", None, "kv"),
    )
    return jax.shard_map(body, mesh=mesh, in_specs=in_specs, out_specs=out_specs, check_vma=False)
```

```python
import math

import jax
import jax.numpy as jnp
from jax import lax
from jax.experimental import pallas as pl
from jax.experimental.pallas import tpu as pltpu
from jax.sharding import PartitionSpec as P


HEAD_SIZE = 128
MASKED = -1e30
SLOTS = 2
EXP2_SCALE = math.log2(math.e) / math.sqrt(HEAD_SIZE)


SMEM = pl.BlockSpec(memory_space=pltpu.SMEM)
VMEM = pl.BlockSpec(memory_space=pltpu.VMEM)
ANY = pl.BlockSpec(memory_space=pl.ANY)


def partner(index, turn, count):
    if count & (count - 1) == 0:
        return index ^ turn
    return (index + turn) % count


def partner_of(index, turn, count):
    if count & (count - 1) == 0:
        return jnp.bitwise_xor(index, turn)
    return lax.rem(index + turn, count)


def source_of(index, turn, count):
    if count & (count - 1) == 0:
        return jnp.bitwise_xor(index, turn)
    return lax.rem(index - turn + count, count)


def split_heads_kernel(keys_ref, values_ref, *message_refs):
    rows = keys_ref.shape[1]
    for head, message_ref in enumerate(message_refs):
        columns = pl.ds(head * HEAD_SIZE, HEAD_SIZE)
        message_ref[:rows, :] = keys_ref[0, :, columns]
        message_ref[rows:, :] = values_ref[0, :, columns]


def split_heads(key_rows, values):
    rows, width = key_rows.shape[1:]
    message = jax.ShapeDtypeStruct((2 * rows, HEAD_SIZE), key_rows.dtype)
    return pl.pallas_call(
        split_heads_kernel,
        out_shape=[message] * (width // HEAD_SIZE),
        in_specs=[VMEM] * 2,
        out_specs=[VMEM] * (width // HEAD_SIZE),
        name="split_heads",
    )(key_rows, values)


def stage_kernel(*refs):
    refs[-1][...] = jnp.zeros_like(refs[-1])


def stage(plan, *arrays):
    return pl.pallas_call(
        stage_kernel,
        out_shape=jax.ShapeDtypeStruct((8, HEAD_SIZE), jnp.float32),
        in_specs=[SMEM] + [ANY] * len(arrays),
        out_specs=VMEM,
        compiler_params=pltpu.CompilerParams(vmem_limit_bytes=2**20),
        name="stage",
    )(plan, *arrays)


def exchange(parts):
    count = lax.axis_size("seq")
    received = []
    for turn in range(1, count):
        route = [(i, partner(i, turn, count)) for i in range(count)]
        received.append(lax.ppermute(parts[turn - 1], "seq", route))
    return received


def gather_turns(message):
    return [message] + exchange([message] * (lax.axis_size("seq") - 1))


def attend_kernel(plan_ref, queries_ref, *refs, count, column, page_tokens):
    block_refs = refs[:count]
    context_ref = refs[count + 1]
    query_ref, held_ref, bias_ref, score_ref, max_ref, sum_ref, acc_ref, sems = refs[count + 2 :]
    rows, width = query_ref.shape
    heads = width // HEAD_SIZE
    pages = rows // page_tokens
    own = lax.axis_index("seq")
    requests = plan_ref.shape[1] - count
    own_block = plan_ref[0, requests + own]

    first_start = jnp.int32(0)
    start = jnp.int32(0)
    starts = []
    for request in range(requests):
        starts.append(start)
        first_start = jnp.where(own_block * pages >= start, start, first_start)
        start = start + plan_ref[0, request]

    def needed(turn):
        block = plan_ref[0, requests + source_of(own, turn, count)]
        return block, (block < own_block) & ((block + 1) * pages > first_start)

    query_copy = pltpu.make_async_copy(
        queries_ref.at[0, :, pl.ds(column, width)], query_ref, sems.at[count]
    )
    copies = [
        pltpu.make_async_copy(block_refs[turn], held_ref.at[turn], sems.at[turn])
        for turn in range(count)
    ]
    copies[0].start()
    query_copy.start()
    for turn in range(1, count):
        pl.when(needed(turn)[1])(copies[turn].start)

    row_page = own_block * pages + lax.broadcasted_iota(jnp.int32, (rows, 1), 0) // page_tokens
    row_start = jnp.zeros((rows, 1), jnp.int32)
    for start in starts:
        row_start = jnp.where(row_page >= start, start, row_start)
    row_start = row_start * page_tokens
    row = lax.broadcasted_iota(jnp.int32, (rows, rows), 0)
    key = lax.broadcasted_iota(jnp.int32, (rows, rows), 1)

    def score(turn, head, before):
        scores = (
            lax.dot_general(
                query_ref[:, head * HEAD_SIZE : (head + 1) * HEAD_SIZE],
                held_ref[turn, :rows, :],
                (((1,), (1,)), ((), ())),
                preferred_element_type=jnp.float32,
            )
            + bias_ref[...]
        )
        score_ref[head % SLOTS] = scores
        top = jnp.broadcast_to(jnp.max(scores, axis=1, keepdims=True), (rows, HEAD_SIZE))
        return top if before is None else jnp.maximum(before, top)

    def weigh(turn, head, top):
        total = jnp.zeros((rows, HEAD_SIZE), jnp.float32)
        pieces = []
        for piece in range(rows // HEAD_SIZE):
            scores = score_ref[head % SLOTS, :, piece * HEAD_SIZE : (piece + 1) * HEAD_SIZE]
            weight = jnp.exp2((scores - top) * EXP2_SCALE)
            total = total + weight
            pieces.append(weight.astype(jnp.bfloat16))
        weights = jnp.concatenate(pieces, axis=1)
        return total, jnp.dot(
            weights, held_ref[turn, rows:, :], preferred_element_type=jnp.float32
        )

    def first_block(head, top):
        total, mixed = weigh(0, head, top)
        max_ref[head] = top
        sum_ref[head] = total
        acc_ref[head] = mixed

    def later_block(turn, head, top):
        total, mixed = weigh(turn, head, top)
        rescale = jnp.exp2((max_ref[head] - top) * EXP2_SCALE)
        max_ref[head] = top
        sum_ref[head] = sum_ref[head] * rescale + total
        acc_ref[head] = acc_ref[head] * rescale + mixed

    allowed = (key >= row_start - own_block * rows) & (key <= row)
    bias_ref[...] = jnp.where(allowed, 0.0, MASKED)
    copies[0].wait()
    query_copy.wait()
    tops = [score(0, 0, None)]
    for head in range(heads):
        if head + 1 < heads:
            tops.append(score(0, head + 1, None))
        first_block(head, tops[head])

    for turn in range(1, count):
        block, wanted = needed(turn)

        @pl.when(wanted)
        def _():
            bias_ref[...] = jnp.where(key >= row_start - block * rows, 0.0, MASKED)
            copies[turn].wait()
            tops = [score(turn, 0, max_ref[0])]
            for head in range(heads):
                if head + 1 < heads:
                    tops.append(score(turn, head + 1, max_ref[head + 1]))
                later_block(turn, head, tops[head])

    for head in range(heads):
        total = jnp.sum(sum_ref[head], axis=1, keepdims=True)
        context_ref[0, :, head * HEAD_SIZE : (head + 1) * HEAD_SIZE] = (
            acc_ref[head] * (1.0 / total)
        ).astype(context_ref.dtype)


def attend(plan, queries, blocks, staged, first, group, page_tokens):
    rows = queries.shape[1]
    count = len(blocks)
    width = group * HEAD_SIZE
    pairs = group * rows * rows * (count + 1) // 2

    def kernel(*refs):
        attend_kernel(
            *refs, count=count, column=first * HEAD_SIZE, page_tokens=page_tokens
        )

    return pl.pallas_call(
        kernel,
        out_shape=jax.ShapeDtypeStruct((1, rows, width), queries.dtype),
        in_specs=[SMEM] + [ANY] * (count + 2),
        out_specs=VMEM,
        scratch_shapes=[
            pltpu.VMEM((rows, width), queries.dtype),
            pltpu.VMEM((count, 2 * rows, HEAD_SIZE), queries.dtype),
            pltpu.VMEM((rows, rows), jnp.float32),
            pltpu.VMEM((SLOTS, rows, rows), jnp.float32),
            pltpu.VMEM((group, rows, HEAD_SIZE), jnp.float32),
            pltpu.VMEM((group, rows, HEAD_SIZE), jnp.float32),
            pltpu.VMEM((group, rows, HEAD_SIZE), jnp.float32),
            pltpu.SemaphoreType.DMA((count + 1,)),
        ],
        compiler_params=pltpu.CompilerParams(vmem_limit_bytes=16 * 2**20),
        cost_estimate=pl.CostEstimate(
            flops=4 * pairs * HEAD_SIZE,
            bytes_accessed=2 * 2 * rows * width + count * 4 * rows * HEAD_SIZE,
            transcendentals=pairs,
        ),
        name="attend",
    )(plan, queries, *blocks, staged)


def for_owner(order_ref, owner_ref, source, owner, pages, act):
    block = order_ref[0, source]

    def page_step(page, rank):
        wanted = owner_ref[block * pages + page] == owner
        pl.when(wanted)(lambda: act(page, rank))
        return rank + wanted.astype(jnp.int32)

    lax.fori_loop(0, pages, page_step, jnp.int32(0))


def page_rows(page, page_tokens, base=0):
    return pl.ds(pl.multiple_of(base + page * page_tokens, page_tokens), page_tokens)


def pack_kernel(order_ref, owner_ref, message_ref, *part_refs, page_tokens):
    count = len(part_refs) + 1
    rows = message_ref.shape[0] // 2
    half = part_refs[0].shape[0] // 2
    own = lax.axis_index("seq")
    for turn in range(1, count):
        part_ref = part_refs[turn - 1]
        part_ref[...] = jnp.zeros_like(part_ref)

        def act(page, rank):
            for base, part_base in ((0, 0), (rows, half)):
                part_ref[page_rows(rank, page_tokens, part_base), :] = message_ref[
                    page_rows(page, page_tokens, base), :
                ]

        owner = partner_of(own, turn, count)
        for_owner(order_ref, owner_ref, own, owner, rows // page_tokens, act)


def pack_pages(block_order, owners, message, slots, page_tokens):
    count = block_order.shape[1]
    part = jax.ShapeDtypeStruct((2 * slots * page_tokens, HEAD_SIZE), message.dtype)

    def kernel(*refs):
        pack_kernel(*refs, page_tokens=page_tokens)

    return pl.pallas_call(
        kernel,
        out_shape=[part] * (count - 1),
        in_specs=[SMEM, SMEM, VMEM],
        out_specs=[VMEM] * (count - 1),
        name="pack_pages",
    )(block_order, owners, message)


def scatter_kernel(order_ref, owner_ref, *refs, columns, page_tokens, slots):
    keys_ref, values_ref = refs[-2:]
    keys_ref[...] = jnp.zeros_like(keys_ref)
    values_ref[...] = jnp.zeros_like(values_ref)
    own = lax.axis_index("seq")
    count = order_ref.shape[1]
    for block_ref, (head, turn) in zip(refs[:-2], columns):
        rows = block_ref.shape[0] // 2
        source = source_of(own, turn, count)
        lanes = pl.ds(head * HEAD_SIZE, HEAD_SIZE)

        def act(page, rank):
            put = page_rows(source * slots + rank, page_tokens)
            keys_ref[0, 0, put, lanes] = block_ref[page_rows(page, page_tokens), :]
            values_ref[0, 0, put, lanes] = block_ref[page_rows(page, page_tokens, rows), :]

        for_owner(order_ref, owner_ref, source, own, rows // page_tokens, act)


def scatter_pages(block_order, owners, blocks, columns, width, page_tokens, slots):
    count = block_order.shape[1]
    cache = jax.ShapeDtypeStruct((1, 1, count * slots * page_tokens, width), blocks[0].dtype)

    def kernel(*refs):
        scatter_kernel(*refs, columns=columns, page_tokens=page_tokens, slots=slots)

    return pl.pallas_call(
        kernel,
        out_shape=[cache, cache],
        in_specs=[SMEM, SMEM] + [VMEM] * len(blocks),
        out_specs=[VMEM, VMEM],
        name="scatter_pages",
    )(block_order, owners, *blocks)


def land_kernel(keys_in_ref, values_in_ref, *refs, head):
    keys_ref, values_ref, sems = refs[-3:]
    part_refs = refs[:-3]
    count = len(part_refs) + 1
    half = part_refs[0].shape[0] // 2
    own = lax.axis_index("seq")
    lanes = pl.ds(head * HEAD_SIZE, HEAD_SIZE)
    copies = []
    for turn in range(1, count):
        source = source_of(own, turn, count)
        put = pl.ds(pl.multiple_of(source * half, half), half)
        for side, cache_ref in enumerate((keys_ref, values_ref)):
            copies.append(
                pltpu.make_async_copy(
                    part_refs[turn - 1].at[pl.ds(side * half, half), :],
                    cache_ref.at[0, 0, put, lanes],
                    sems.at[2 * (turn - 1) + side],
                )
            )
    for copy in copies:
        copy.start()
    for copy in copies:
        copy.wait()


def land_pages(cache_keys, cache_values, parts, head):
    def kernel(*refs):
        land_kernel(*refs, head=head)

    return pl.pallas_call(
        kernel,
        out_shape=[
            jax.ShapeDtypeStruct(cache.shape, cache.dtype) for cache in (cache_keys, cache_values)
        ],
        in_specs=[ANY] * (2 + len(parts)),
        out_specs=[ANY, ANY],
        scratch_shapes=[pltpu.SemaphoreType.DMA((2 * len(parts),))],
        input_output_aliases={0: 0, 1: 1},
        compiler_params=pltpu.CompilerParams(vmem_limit_bytes=48 * 2**20),
        name="land_pages",
    )(cache_keys, cache_values, *parts)


def body(queries, key_rows, values, lengths, block_order, page_owner):
    count = lax.axis_size("seq")
    sections = lax.axis_size("section")
    rows = key_rows.shape[1]
    width = key_rows.shape[2]
    kv_heads = width // HEAD_SIZE
    group = queries.shape[2] // width
    kept = kv_heads - kv_heads // 2
    device_pages = page_owner.shape[1] // count
    page_tokens = rows // device_pages
    slots = max(2, 2 * device_pages // count)
    owners = page_owner.reshape(page_owner.shape[1])
    onward = [(i, (i + 1) % sections) for i in range(sections)]

    def hand_on(array):
        return lax.ppermute(array, "section", onward)

    messages = split_heads(key_rows, values)
    plan = jnp.concatenate([lengths, block_order], axis=1)
    gathered = [gather_turns(messages[head]) for head in range(kept)]
    swapped = [hand_on(messages[head]) for head in range(kept, kv_heads)]
    other_plan = hand_on(plan)
    other_queries = [
        hand_on(queries[:, :, head * group * HEAD_SIZE : (head + 1) * group * HEAD_SIZE])
        for head in range(kept, kv_heads)
    ]
    gathered += [gather_turns(message) for message in swapped]
    parts = []
    for head in range(kept, kv_heads):
        packed = pack_pages(block_order, owners, messages[head], slots, page_tokens)
        parts.append(exchange(packed))
    staged = stage(plan, queries, *messages[:kept])
    handed = []
    for head in range(kept):
        context = attend(plan, queries, gathered[head], staged, head * group, group, page_tokens)
        handed.append(hand_on(context))
    for index, head in enumerate(range(kept, kv_heads)):
        handed.append(
            attend(other_plan, other_queries[index], gathered[head], staged, 0, group, page_tokens)
        )
    columns = [(head, turn) for head in range(kept) for turn in range(count)]
    columns += [(head, 0) for head in range(kept, kv_heads)]
    blocks = [gathered[head][turn] if head < kept else messages[head] for head, turn in columns]
    cache = scatter_pages(block_order, owners, blocks, columns, width, page_tokens, slots)
    for index, head in enumerate(range(kept, kv_heads)):
        cache = land_pages(*cache, parts[index], head)
    return (jnp.concatenate(handed, axis=2), *cache)


def solution(mesh):
    in_specs = (
        P(("groups", "section"), "seq", "kv"),
        P(("groups", "section"), "seq", "kv"),
        P(("groups", "section"), "seq", "kv"),
        P(("groups", "section"), None),
        P(("groups", "section"), None),
        P(("groups", "section"), None, None),
    )
    out_specs = (
        P(("groups", "section"), "seq", "kv"),
        P(("groups", "section"), "seq", None, "kv"),
        P(("groups", "section"), "seq", None, "kv"),
    )
    return jax.shard_map(body, mesh=mesh, in_specs=in_specs, out_specs=out_specs, check_vma=False)
```

```python
import math

import jax
import jax.numpy as jnp
from jax import lax
from jax.experimental import pallas as pl
from jax.experimental.pallas import tpu as pltpu
from jax.sharding import PartitionSpec as P


HEAD_SIZE = 128
MASKED = -1e30
SLOTS = 2
EXP2_SCALE = math.log2(math.e) / math.sqrt(HEAD_SIZE)


SMEM = pl.BlockSpec(memory_space=pltpu.SMEM)
VMEM = pl.BlockSpec(memory_space=pltpu.VMEM)
ANY = pl.BlockSpec(memory_space=pl.ANY)


def partner(index, turn, count):
    if count & (count - 1) == 0:
        return index ^ turn
    return (index + turn) % count


def partner_of(index, turn, count):
    if count & (count - 1) == 0:
        return jnp.bitwise_xor(index, turn)
    return lax.rem(index + turn, count)


def source_of(index, turn, count):
    if count & (count - 1) == 0:
        return jnp.bitwise_xor(index, turn)
    return lax.rem(index - turn + count, count)


def split_heads_kernel(keys_ref, values_ref, *message_refs):
    rows = keys_ref.shape[1]
    for head, message_ref in enumerate(message_refs):
        columns = pl.ds(head * HEAD_SIZE, HEAD_SIZE)
        message_ref[:rows, :] = keys_ref[0, :, columns]
        message_ref[rows:, :] = values_ref[0, :, columns]


def split_heads(key_rows, values):
    rows, width = key_rows.shape[1:]
    message = jax.ShapeDtypeStruct((2 * rows, HEAD_SIZE), key_rows.dtype)
    return pl.pallas_call(
        split_heads_kernel,
        out_shape=[message] * (width // HEAD_SIZE),
        in_specs=[VMEM] * 2,
        out_specs=[VMEM] * (width // HEAD_SIZE),
        name="split_heads",
    )(key_rows, values)


def stage_kernel(*refs):
    refs[-1][...] = jnp.zeros_like(refs[-1])


def stage(plan, *arrays):
    return pl.pallas_call(
        stage_kernel,
        out_shape=jax.ShapeDtypeStruct((8, HEAD_SIZE), jnp.float32),
        in_specs=[SMEM] + [ANY] * len(arrays),
        out_specs=VMEM,
        compiler_params=pltpu.CompilerParams(vmem_limit_bytes=2**20),
        name="stage",
    )(plan, *arrays)


def exchange(parts):
    count = lax.axis_size("seq")
    received = []
    for turn in range(1, count):
        route = [(i, partner(i, turn, count)) for i in range(count)]
        received.append(lax.ppermute(parts[turn - 1], "seq", route))
    return received


def gather_turns(message):
    return [message] + exchange([message] * (lax.axis_size("seq") - 1))


def attend_kernel(plan_ref, queries_ref, *refs, count, column, page_tokens):
    block_refs = refs[:count]
    context_ref = refs[count + 1]
    query_ref, held_ref, bias_ref, score_ref, max_ref, sum_ref, acc_ref, sems = refs[count + 2 :]
    rows, width = query_ref.shape
    heads = width // HEAD_SIZE
    pages = rows // page_tokens
    own = lax.axis_index("seq")
    requests = plan_ref.shape[1] - count
    own_block = plan_ref[0, requests + own]

    first_start = jnp.int32(0)
    start = jnp.int32(0)
    starts = []
    for request in range(requests):
        starts.append(start)
        first_start = jnp.where(own_block * pages >= start, start, first_start)
        start = start + plan_ref[0, request]

    def needed(turn):
        block = plan_ref[0, requests + source_of(own, turn, count)]
        return block, (block < own_block) & ((block + 1) * pages > first_start)

    query_copy = pltpu.make_async_copy(
        queries_ref.at[0, :, pl.ds(column, width)], query_ref, sems.at[count]
    )
    copies = [
        pltpu.make_async_copy(block_refs[turn], held_ref.at[turn], sems.at[turn])
        for turn in range(count)
    ]
    copies[0].start()
    query_copy.start()
    for turn in range(1, count):
        pl.when(needed(turn)[1])(copies[turn].start)

    row_page = own_block * pages + lax.broadcasted_iota(jnp.int32, (rows, 1), 0) // page_tokens
    row_start = jnp.zeros((rows, 1), jnp.int32)
    for start in starts:
        row_start = jnp.where(row_page >= start, start, row_start)
    row_start = row_start * page_tokens
    row = lax.broadcasted_iota(jnp.int32, (rows, rows), 0)
    key = lax.broadcasted_iota(jnp.int32, (rows, rows), 1)

    def score(turn, head, before):
        scores = (
            lax.dot_general(
                query_ref[:, head * HEAD_SIZE : (head + 1) * HEAD_SIZE],
                held_ref[turn, :rows, :],
                (((1,), (1,)), ((), ())),
                preferred_element_type=jnp.float32,
            )
            + bias_ref[...]
        )
        score_ref[head % SLOTS] = scores
        top = jnp.broadcast_to(jnp.max(scores, axis=1, keepdims=True), (rows, HEAD_SIZE))
        return top if before is None else jnp.maximum(before, top)

    def weigh(turn, head, top):
        total = jnp.zeros((rows, HEAD_SIZE), jnp.float32)
        pieces = []
        for piece in range(rows // HEAD_SIZE):
            scores = score_ref[head % SLOTS, :, piece * HEAD_SIZE : (piece + 1) * HEAD_SIZE]
            weight = jnp.exp2((scores - top) * EXP2_SCALE)
            total = total + weight
            pieces.append(weight.astype(jnp.bfloat16))
        weights = jnp.concatenate(pieces, axis=1)
        return total, jnp.dot(
            weights, held_ref[turn, rows:, :], preferred_element_type=jnp.float32
        )

    def first_block(head, top):
        total, mixed = weigh(0, head, top)
        max_ref[head] = top
        sum_ref[head] = total
        acc_ref[head] = mixed

    def later_block(turn, head, top):
        total, mixed = weigh(turn, head, top)
        rescale = jnp.exp2((max_ref[head] - top) * EXP2_SCALE)
        max_ref[head] = top
        sum_ref[head] = sum_ref[head] * rescale + total
        acc_ref[head] = acc_ref[head] * rescale + mixed

    allowed = (key >= row_start - own_block * rows) & (key <= row)
    bias_ref[...] = jnp.where(allowed, 0.0, MASKED)
    copies[0].wait()
    query_copy.wait()
    tops = [score(0, 0, None)]
    for head in range(heads):
        if head + 1 < heads:
            tops.append(score(0, head + 1, None))
        first_block(head, tops[head])

    for turn in range(1, count):
        block, wanted = needed(turn)

        @pl.when(wanted)
        def _():
            bias_ref[...] = jnp.where(key >= row_start - block * rows, 0.0, MASKED)
            copies[turn].wait()
            tops = [score(turn, 0, max_ref[0])]
            for head in range(heads):
                if head + 1 < heads:
                    tops.append(score(turn, head + 1, max_ref[head + 1]))
                later_block(turn, head, tops[head])

    for head in range(heads):
        total = jnp.sum(sum_ref[head], axis=1, keepdims=True)
        context_ref[0, :, head * HEAD_SIZE : (head + 1) * HEAD_SIZE] = (
            acc_ref[head] * (1.0 / total)
        ).astype(context_ref.dtype)


def attend(plan, queries, blocks, staged, first, group, page_tokens):
    rows = queries.shape[1]
    count = len(blocks)
    width = group * HEAD_SIZE
    pairs = group * rows * rows * (count + 1) // 2

    def kernel(*refs):
        attend_kernel(
            *refs, count=count, column=first * HEAD_SIZE, page_tokens=page_tokens
        )

    return pl.pallas_call(
        kernel,
        out_shape=jax.ShapeDtypeStruct((1, rows, width), queries.dtype),
        in_specs=[SMEM] + [ANY] * (count + 2),
        out_specs=VMEM,
        scratch_shapes=[
            pltpu.VMEM((rows, width), queries.dtype),
            pltpu.VMEM((count, 2 * rows, HEAD_SIZE), queries.dtype),
            pltpu.VMEM((rows, rows), jnp.float32),
            pltpu.VMEM((SLOTS, rows, rows), jnp.float32),
            pltpu.VMEM((group, rows, HEAD_SIZE), jnp.float32),
            pltpu.VMEM((group, rows, HEAD_SIZE), jnp.float32),
            pltpu.VMEM((group, rows, HEAD_SIZE), jnp.float32),
            pltpu.SemaphoreType.DMA((count + 1,)),
        ],
        compiler_params=pltpu.CompilerParams(vmem_limit_bytes=16 * 2**20),
        cost_estimate=pl.CostEstimate(
            flops=4 * pairs * HEAD_SIZE,
            bytes_accessed=2 * 2 * rows * width + count * 4 * rows * HEAD_SIZE,
            transcendentals=pairs,
        ),
        name="attend",
    )(plan, queries, *blocks, staged)


def page_rows(page, page_tokens, base=0):
    start = base + page * page_tokens
    return pl.ds(start if isinstance(start, int) else pl.multiple_of(start, page_tokens), page_tokens)


def pack_kernel(order_ref, owner_ref, message_ref, *refs, page_tokens):
    part_refs, buffer_ref = refs[:-1], refs[-1]
    count = len(part_refs) + 1
    rows = message_ref.shape[0] // 2
    half = part_refs[0].shape[0] // 2
    pages = rows // page_tokens
    own = lax.axis_index("seq")
    block = order_ref[0, own]
    buffer_ref[...] = jnp.zeros_like(buffer_ref)
    taken = [jnp.int32(0)] * count
    for page in range(pages):
        owner = owner_ref[block * pages + page]
        rank = jnp.int32(0)
        for index in range(count):
            same = owner == index
            rank = jnp.where(same, taken[index], rank)
            taken[index] = taken[index] + same.astype(jnp.int32)
        for base, part_base in ((0, 0), (rows, half)):
            buffer_ref[owner, page_rows(rank, page_tokens, part_base), :] = message_ref[
                page_rows(page, page_tokens, base), :
            ]
    for turn in range(1, count):
        part_refs[turn - 1][...] = buffer_ref[partner_of(own, turn, count)]


def pack_pages(block_order, owners, message, slots, page_tokens):
    count = block_order.shape[1]
    shape = (2 * slots * page_tokens, HEAD_SIZE)
    part = jax.ShapeDtypeStruct(shape, message.dtype)

    def kernel(*refs):
        pack_kernel(*refs, page_tokens=page_tokens)

    return pl.pallas_call(
        kernel,
        out_shape=[part] * (count - 1),
        in_specs=[SMEM, SMEM, VMEM],
        out_specs=[VMEM] * (count - 1),
        scratch_shapes=[pltpu.VMEM((count, *shape), message.dtype)],
        name="pack_pages",
    )(block_order, owners, message)


def scatter_kernel(order_ref, owner_ref, *refs, columns, page_tokens, slots):
    keys_ref, values_ref, held_keys_ref, held_values_ref = refs[-4:]
    total = keys_ref.shape[2]
    held_keys_ref[...] = jnp.zeros_like(held_keys_ref)
    held_values_ref[...] = jnp.zeros_like(held_values_ref)
    own = lax.axis_index("seq")
    count = order_ref.shape[1]
    for turn in range(count):
        source = source_of(own, turn, count)
        block = order_ref[0, source]
        heads = [(ref, head) for ref, (head, at) in zip(refs[:-4], columns) if at == turn]
        rows = heads[0][0].shape[0] // 2
        pages = rows // page_tokens
        rank = source * slots
        for page in range(pages):
            mine = owner_ref[block * pages + page] == own
            put = page_rows(jnp.where(mine, rank, total // page_tokens), page_tokens)
            rank = rank + mine.astype(jnp.int32)
            for block_ref, head in heads:
                lanes = pl.ds(head * HEAD_SIZE, HEAD_SIZE)
                held_keys_ref[put, lanes] = block_ref[page_rows(page, page_tokens), :]
                held_values_ref[put, lanes] = block_ref[page_rows(page, page_tokens, rows), :]
    keys_ref[0, 0] = held_keys_ref[:total, :]
    values_ref[0, 0] = held_values_ref[:total, :]


def scatter_pages(block_order, owners, blocks, columns, width, page_tokens, slots):
    count = block_order.shape[1]
    total = count * slots * page_tokens
    cache = jax.ShapeDtypeStruct((1, 1, total, width), blocks[0].dtype)

    def kernel(*refs):
        scatter_kernel(*refs, columns=columns, page_tokens=page_tokens, slots=slots)

    return pl.pallas_call(
        kernel,
        out_shape=[cache, cache],
        in_specs=[SMEM, SMEM] + [VMEM] * len(blocks),
        out_specs=[VMEM, VMEM],
        scratch_shapes=[pltpu.VMEM((total + page_tokens, width), blocks[0].dtype)] * 2,
        name="scatter_pages",
    )(block_order, owners, *blocks)


def finish_kernel(*refs, contexts, heads):
    count = lax.axis_size("seq")
    context_refs = refs[2 : 2 + contexts]
    part_refs = refs[2 + contexts : -4]
    keys_ref, values_ref, handed_ref, sems = refs[-4:]
    half = part_refs[0].shape[0] // 2
    own = lax.axis_index("seq")
    copies = []
    start = 0
    for context_ref in context_refs:
        width = context_ref.shape[2]
        copies.append((context_ref, handed_ref.at[:, :, pl.ds(start, width)]))
        start += width
    for index, part_ref in enumerate(part_refs):
        lanes = pl.ds(heads[index // (count - 1)] * HEAD_SIZE, HEAD_SIZE)
        source = source_of(own, index % (count - 1) + 1, count)
        put = pl.ds(pl.multiple_of(source * half, half), half)
        for side, cache_ref in enumerate((keys_ref, values_ref)):
            copies.append(
                (part_ref.at[pl.ds(side * half, half), :], cache_ref.at[0, 0, put, lanes])
            )
    copies = [
        pltpu.make_async_copy(source, target, sems.at[index])
        for index, (source, target) in enumerate(copies)
    ]
    for copy in copies:
        copy.start()
    for copy in copies:
        copy.wait()


def finish(cache_keys, cache_values, contexts, parts, heads):
    rows = contexts[0].shape[1]
    width = sum(context.shape[2] for context in contexts)

    def kernel(*refs):
        finish_kernel(*refs, contexts=len(contexts), heads=heads)

    outputs = [
        jax.ShapeDtypeStruct(cache.shape, cache.dtype) for cache in (cache_keys, cache_values)
    ]
    outputs.append(jax.ShapeDtypeStruct((1, rows, width), contexts[0].dtype))
    return pl.pallas_call(
        kernel,
        out_shape=outputs,
        in_specs=[ANY] * (2 + len(contexts) + len(parts)),
        out_specs=[ANY] * 3,
        scratch_shapes=[pltpu.SemaphoreType.DMA((len(contexts) + 2 * len(parts),))],
        input_output_aliases={0: 0, 1: 1},
        compiler_params=pltpu.CompilerParams(vmem_limit_bytes=48 * 2**20),
        name="finish",
    )(cache_keys, cache_values, *contexts, *parts)


def body(queries, key_rows, values, lengths, block_order, page_owner):
    count = lax.axis_size("seq")
    sections = lax.axis_size("section")
    rows = key_rows.shape[1]
    width = key_rows.shape[2]
    kv_heads = width // HEAD_SIZE
    group = queries.shape[2] // width
    kept = kv_heads - kv_heads // 2
    device_pages = page_owner.shape[1] // count
    page_tokens = rows // device_pages
    slots = max(2, 2 * device_pages // count)
    owners = page_owner.reshape(page_owner.shape[1])
    onward = [(i, (i + 1) % sections) for i in range(sections)]

    def hand_on(array):
        return lax.ppermute(array, "section", onward)

    messages = split_heads(key_rows, values)
    plan = jnp.concatenate([lengths, block_order], axis=1)
    gathered = [gather_turns(messages[head]) for head in range(kept)]
    swapped = [hand_on(messages[head]) for head in range(kept, kv_heads)]
    other_plan = hand_on(plan)
    other_queries = [
        hand_on(queries[:, :, head * group * HEAD_SIZE : (head + 1) * group * HEAD_SIZE])
        for head in range(kept, kv_heads)
    ]
    gathered += [gather_turns(message) for message in swapped]
    parts = []
    for head in range(kept, kv_heads):
        packed = pack_pages(block_order, owners, messages[head], slots, page_tokens)
        parts += exchange(packed)
    staged = stage(plan, queries, *messages[:kept])
    handed = []
    for head in range(kept):
        context = attend(plan, queries, gathered[head], staged, head * group, group, page_tokens)
        handed.append(hand_on(context))
    for index, head in enumerate(range(kept, kv_heads)):
        handed.append(
            attend(other_plan, other_queries[index], gathered[head], staged, 0, group, page_tokens)
        )
    columns = [(head, turn) for head in range(kept) for turn in range(count)]
    columns += [(head, 0) for head in range(kept, kv_heads)]
    blocks = [gathered[head][turn] if head < kept else messages[head] for head, turn in columns]
    cache = scatter_pages(block_order, owners, blocks, columns, width, page_tokens, slots)
    cache_keys, cache_values, context = finish(*cache, handed, parts, list(range(kept, kv_heads)))
    return (context, cache_keys, cache_values)


def solution(mesh):
    in_specs = (
        P(("groups", "section"), "seq", "kv"),
        P(("groups", "section"), "seq", "kv"),
        P(("groups", "section"), "seq", "kv"),
        P(("groups", "section"), None),
        P(("groups", "section"), None),
        P(("groups", "section"), None, None),
    )
    out_specs = (
        P(("groups", "section"), "seq", "kv"),
        P(("groups", "section"), "seq", None, "kv"),
        P(("groups", "section"), "seq", None, "kv"),
    )
    return jax.shard_map(body, mesh=mesh, in_specs=in_specs, out_specs=out_specs, check_vma=False)
```

```python
import math

import jax
import jax.numpy as jnp
from jax import lax
from jax.experimental import pallas as pl
from jax.experimental.pallas import tpu as pltpu
from jax.sharding import PartitionSpec as P


HEAD_SIZE = 128
MASKED = -1e30
SLOTS = 2
EXP2_SCALE = math.log2(math.e) / math.sqrt(HEAD_SIZE)


SMEM = pl.BlockSpec(memory_space=pltpu.SMEM)
VMEM = pl.BlockSpec(memory_space=pltpu.VMEM)
ANY = pl.BlockSpec(memory_space=pl.ANY)


def partner(index, turn, count):
    if count & (count - 1) == 0:
        return index ^ turn
    return (index + turn) % count


def partner_of(index, turn, count):
    if count & (count - 1) == 0:
        return jnp.bitwise_xor(index, turn)
    return lax.rem(index + turn, count)


def source_of(index, turn, count):
    if count & (count - 1) == 0:
        return jnp.bitwise_xor(index, turn)
    return lax.rem(index - turn + count, count)


def head_message(key_rows, values, head):
    lanes = slice(head * HEAD_SIZE, (head + 1) * HEAD_SIZE)
    return jnp.concatenate([key_rows[0, :, lanes], values[0, :, lanes]], axis=0)


def stage_kernel(*refs):
    refs[-1][...] = jnp.zeros_like(refs[-1])


def stage(plan, *arrays):
    return pl.pallas_call(
        stage_kernel,
        out_shape=jax.ShapeDtypeStruct((8, HEAD_SIZE), jnp.float32),
        in_specs=[SMEM] + [ANY] * len(arrays),
        out_specs=VMEM,
        compiler_params=pltpu.CompilerParams(vmem_limit_bytes=2**20),
        name="stage",
    )(plan, *arrays)


def exchange(parts):
    count = lax.axis_size("seq")
    received = []
    for turn in range(1, count):
        route = [(i, partner(i, turn, count)) for i in range(count)]
        received.append(lax.ppermute(parts[turn - 1], "seq", route))
    return received


def gather_turns(message):
    return [message] + exchange([message] * (lax.axis_size("seq") - 1))


def attend_kernel(plan_ref, queries_ref, *refs, count, column, page_tokens):
    block_refs = refs[:count]
    context_ref = refs[count + 1]
    query_ref, keys_ref, values_ref, bias_ref, score_ref, max_ref, acc_ref, sems = refs[count + 2 :]
    rows, width = query_ref.shape
    heads = width // HEAD_SIZE
    pages = rows // page_tokens
    half = rows // 2
    own = lax.axis_index("seq")
    requests = plan_ref.shape[1] - count
    own_block = plan_ref[0, requests + own]

    first_start = jnp.int32(0)
    first_end = jnp.int32(0)
    start = jnp.int32(0)
    starts = []
    for request in range(requests):
        starts.append(start)
        covers = own_block * pages >= start
        first_start = jnp.where(covers, start, first_start)
        start = start + plan_ref[0, request]
        first_end = jnp.where(covers, start, first_end)

    def needed(turn):
        block = plan_ref[0, requests + source_of(own, turn, count)]
        return block, (block < own_block) & ((block + 1) * pages > first_start)

    def start_block(turn):
        copies[turn][0].start()
        copies[turn][1].start()

    def wait_block(turn):
        copies[turn][0].wait()
        copies[turn][1].wait()

    query_copy = pltpu.make_async_copy(
        queries_ref.at[0, :, pl.ds(column, width)], query_ref, sems.at[2 * count]
    )
    copies = [
        (
            pltpu.make_async_copy(
                block_refs[turn].at[pl.ds(0, rows), :], keys_ref.at[turn], sems.at[2 * turn]
            ),
            pltpu.make_async_copy(
                block_refs[turn].at[pl.ds(rows, rows), :],
                values_ref.at[turn, :, pl.ds(0, HEAD_SIZE)],
                sems.at[2 * turn + 1],
            ),
        )
        for turn in range(count)
    ]
    start_block(0)
    query_copy.start()
    for turn in range(1, count):
        pl.when(needed(turn)[1])(lambda turn=turn: start_block(turn))

    row_page = own_block * pages + lax.broadcasted_iota(jnp.int32, (rows, 1), 0) // page_tokens
    row_start = jnp.zeros((rows, 1), jnp.int32)
    for start in starts:
        row_start = jnp.where(row_page >= start, start, row_start)
    row_start = row_start * page_tokens
    row = lax.broadcasted_iota(jnp.int32, (rows, rows), 0)
    key = lax.broadcasted_iota(jnp.int32, (rows, rows), 1)
    values_ref[:, :, HEAD_SIZE:] = jnp.ones((count, rows, HEAD_SIZE), values_ref.dtype)

    def score(turn, head, take, keys, first):
        scores = (
            lax.dot_general(
                query_ref[take, head * HEAD_SIZE : (head + 1) * HEAD_SIZE],
                keys_ref[turn, :keys, :],
                (((1,), (1,)), ((), ())),
                preferred_element_type=jnp.float32,
            )
            + bias_ref[take, :keys]
        )
        score_ref[head % SLOTS, :, :keys] = scores
        top = jnp.max(scores, axis=1, keepdims=True)
        top = jnp.broadcast_to(top, (scores.shape[0], HEAD_SIZE))
        return top if first else jnp.maximum(max_ref[head, take], top)

    def weigh(turn, head, keys, top):
        pieces = []
        for piece in range(keys // HEAD_SIZE):
            scores = score_ref[head % SLOTS, :, piece * HEAD_SIZE : (piece + 1) * HEAD_SIZE]
            pieces.append(jnp.exp2((scores - top) * EXP2_SCALE).astype(jnp.bfloat16))
        weights = pieces[0] if len(pieces) == 1 else jnp.concatenate(pieces, axis=1)
        return jnp.dot(weights, values_ref[turn, :keys, :], preferred_element_type=jnp.float32)

    def visit(turn, take, keys, first):
        tops = [score(turn, 0, take, keys, first)]
        for head in range(heads):
            if head + 1 < heads:
                tops.append(score(turn, head + 1, take, keys, first))
            mixed = weigh(turn, head, keys, tops[head])
            if not first:
                rescale = jnp.exp2((max_ref[head, take] - tops[head]) * EXP2_SCALE)
                mixed = acc_ref[head, take] * jnp.concatenate([rescale, rescale], axis=1) + mixed
            acc_ref[head, take] = mixed
            max_ref[head, take] = tops[head]

    allowed = (key >= row_start - own_block * rows) & (key <= row)
    bias_ref[...] = jnp.where(allowed, 0.0, MASKED)
    wait_block(0)
    query_copy.wait()
    visit(0, slice(0, half), half, True)
    visit(0, slice(half, rows), rows, True)

    for turn in range(1, count):
        block, wanted = needed(turn)

        @pl.when(wanted)
        def _():
            bias_ref[...] = jnp.where(key >= row_start - block * rows, 0.0, MASKED)
            wait_block(turn)
            visit(turn, slice(0, half), rows, False)

            @pl.when((first_end - own_block * pages) * page_tokens > half)
            def _():
                visit(turn, slice(half, rows), rows, False)

    for head in range(heads):
        context_ref[0, :, head * HEAD_SIZE : (head + 1) * HEAD_SIZE] = (
            acc_ref[head, :, :HEAD_SIZE] * (1.0 / acc_ref[head, :, HEAD_SIZE:])
        ).astype(context_ref.dtype)


def attend(plan, queries, blocks, staged, first, group, page_tokens):
    rows = queries.shape[1]
    count = len(blocks)
    width = group * HEAD_SIZE
    pairs = group * rows * rows * (count + 1) // 2

    def kernel(*refs):
        attend_kernel(
            *refs, count=count, column=first * HEAD_SIZE, page_tokens=page_tokens
        )

    return pl.pallas_call(
        kernel,
        out_shape=jax.ShapeDtypeStruct((1, rows, width), queries.dtype),
        in_specs=[SMEM] + [ANY] * (count + 2),
        out_specs=VMEM,
        scratch_shapes=[
            pltpu.VMEM((rows, width), queries.dtype),
            pltpu.VMEM((count, rows, HEAD_SIZE), queries.dtype),
            pltpu.VMEM((count, rows, 2 * HEAD_SIZE), queries.dtype),
            pltpu.VMEM((rows, rows), jnp.float32),
            pltpu.VMEM((SLOTS, rows // 2, rows), jnp.float32),
            pltpu.VMEM((group, rows, HEAD_SIZE), jnp.float32),
            pltpu.VMEM((group, rows, 2 * HEAD_SIZE), jnp.float32),
            pltpu.SemaphoreType.DMA((2 * count + 1,)),
        ],
        compiler_params=pltpu.CompilerParams(vmem_limit_bytes=16 * 2**20),
        cost_estimate=pl.CostEstimate(
            flops=4 * pairs * HEAD_SIZE,
            bytes_accessed=2 * 2 * rows * width + count * 4 * rows * HEAD_SIZE,
            transcendentals=pairs,
        ),
        name="attend",
    )(plan, queries, *blocks, staged)


def page_rows(page, page_tokens, base=0):
    start = base + page * page_tokens
    return pl.ds(start if isinstance(start, int) else pl.multiple_of(start, page_tokens), page_tokens)


def pack_kernel(order_ref, owner_ref, message_ref, *refs, page_tokens):
    part_refs, buffer_ref = refs[:-1], refs[-1]
    count = len(part_refs) + 1
    rows = message_ref.shape[0] // 2
    half = part_refs[0].shape[0] // 2
    pages = rows // page_tokens
    own = lax.axis_index("seq")
    block = order_ref[0, own]
    buffer_ref[...] = jnp.zeros_like(buffer_ref)
    taken = [jnp.int32(0)] * count
    for page in range(pages):
        owner = owner_ref[block * pages + page]
        rank = jnp.int32(0)
        for index in range(count):
            same = owner == index
            rank = jnp.where(same, taken[index], rank)
            taken[index] = taken[index] + same.astype(jnp.int32)
        for base, part_base in ((0, 0), (rows, half)):
            buffer_ref[owner, page_rows(rank, page_tokens, part_base), :] = message_ref[
                page_rows(page, page_tokens, base), :
            ]
    for turn in range(1, count):
        part_refs[turn - 1][...] = buffer_ref[partner_of(own, turn, count)]


def pack_pages(block_order, owners, message, slots, page_tokens):
    count = block_order.shape[1]
    shape = (2 * slots * page_tokens, HEAD_SIZE)
    part = jax.ShapeDtypeStruct(shape, message.dtype)

    def kernel(*refs):
        pack_kernel(*refs, page_tokens=page_tokens)

    return pl.pallas_call(
        kernel,
        out_shape=[part] * (count - 1),
        in_specs=[SMEM, SMEM, VMEM],
        out_specs=[VMEM] * (count - 1),
        scratch_shapes=[pltpu.VMEM((count, *shape), message.dtype)],
        name="pack_pages",
    )(block_order, owners, message)


def scatter_kernel(order_ref, owner_ref, *refs, columns, page_tokens, slots):
    keys_ref, values_ref, held_keys_ref, held_values_ref = refs[-4:]
    total = keys_ref.shape[2]
    held_keys_ref[...] = jnp.zeros_like(held_keys_ref)
    held_values_ref[...] = jnp.zeros_like(held_values_ref)
    own = lax.axis_index("seq")
    count = order_ref.shape[1]
    for turn in range(count):
        source = source_of(own, turn, count)
        block = order_ref[0, source]
        heads = [(ref, head) for ref, (head, at) in zip(refs[:-4], columns) if at == turn]
        rows = heads[0][0].shape[0] // 2
        pages = rows // page_tokens
        rank = source * slots
        for page in range(pages):
            mine = owner_ref[block * pages + page] == own
            put = page_rows(jnp.where(mine, rank, total // page_tokens), page_tokens)
            rank = rank + mine.astype(jnp.int32)
            for block_ref, head in heads:
                lanes = pl.ds(head * HEAD_SIZE, HEAD_SIZE)
                held_keys_ref[put, lanes] = block_ref[page_rows(page, page_tokens), :]
                held_values_ref[put, lanes] = block_ref[page_rows(page, page_tokens, rows), :]
    keys_ref[0, 0] = held_keys_ref[:total, :]
    values_ref[0, 0] = held_values_ref[:total, :]


def scatter_pages(block_order, owners, blocks, columns, width, page_tokens, slots):
    count = block_order.shape[1]
    total = count * slots * page_tokens
    cache = jax.ShapeDtypeStruct((1, 1, total, width), blocks[0].dtype)

    def kernel(*refs):
        scatter_kernel(*refs, columns=columns, page_tokens=page_tokens, slots=slots)

    return pl.pallas_call(
        kernel,
        out_shape=[cache, cache],
        in_specs=[SMEM, SMEM] + [VMEM] * len(blocks),
        out_specs=[VMEM, VMEM],
        scratch_shapes=[pltpu.VMEM((total + page_tokens, width), blocks[0].dtype)] * 2,
        name="scatter_pages",
    )(block_order, owners, *blocks)


def finish_kernel(*refs, contexts, heads):
    count = lax.axis_size("seq")
    context_refs = refs[2 : 2 + contexts]
    part_refs = refs[2 + contexts : -4]
    keys_ref, values_ref, handed_ref, sems = refs[-4:]
    half = part_refs[0].shape[0] // 2
    own = lax.axis_index("seq")
    copies = []
    start = 0
    for context_ref in context_refs:
        width = context_ref.shape[2]
        copies.append((context_ref, handed_ref.at[:, :, pl.ds(start, width)]))
        start += width
    for index, part_ref in enumerate(part_refs):
        lanes = pl.ds(heads[index // (count - 1)] * HEAD_SIZE, HEAD_SIZE)
        source = source_of(own, index % (count - 1) + 1, count)
        put = pl.ds(pl.multiple_of(source * half, half), half)
        for side, cache_ref in enumerate((keys_ref, values_ref)):
            copies.append(
                (part_ref.at[pl.ds(side * half, half), :], cache_ref.at[0, 0, put, lanes])
            )
    copies = [
        pltpu.make_async_copy(source, target, sems.at[index])
        for index, (source, target) in enumerate(copies)
    ]
    for copy in copies:
        copy.start()
    for copy in copies:
        copy.wait()


def finish(cache_keys, cache_values, contexts, parts, heads):
    rows = contexts[0].shape[1]
    width = sum(context.shape[2] for context in contexts)

    def kernel(*refs):
        finish_kernel(*refs, contexts=len(contexts), heads=heads)

    outputs = [
        jax.ShapeDtypeStruct(cache.shape, cache.dtype) for cache in (cache_keys, cache_values)
    ]
    outputs.append(jax.ShapeDtypeStruct((1, rows, width), contexts[0].dtype))
    return pl.pallas_call(
        kernel,
        out_shape=outputs,
        in_specs=[ANY] * (2 + len(contexts) + len(parts)),
        out_specs=[ANY] * 3,
        scratch_shapes=[pltpu.SemaphoreType.DMA((len(contexts) + 2 * len(parts),))],
        input_output_aliases={0: 0, 1: 1},
        compiler_params=pltpu.CompilerParams(vmem_limit_bytes=48 * 2**20),
        name="finish",
    )(cache_keys, cache_values, *contexts, *parts)


def body(queries, key_rows, values, lengths, block_order, page_owner):
    count = lax.axis_size("seq")
    sections = lax.axis_size("section")
    rows = key_rows.shape[1]
    width = key_rows.shape[2]
    kv_heads = width // HEAD_SIZE
    group = queries.shape[2] // width
    kept = kv_heads - kv_heads // 2
    device_pages = page_owner.shape[1] // count
    page_tokens = rows // device_pages
    slots = max(2, 2 * device_pages // count)
    owners = page_owner.reshape(page_owner.shape[1])
    onward = [(i, (i + 1) % sections) for i in range(sections)]

    def hand_on(array):
        return lax.ppermute(array, "section", onward)

    messages = [head_message(key_rows, values, head) for head in range(kv_heads)]
    plan = jnp.concatenate([lengths, block_order], axis=1)
    gathered = [gather_turns(messages[head]) for head in range(kept)]
    swapped = [hand_on(messages[head]) for head in range(kept, kv_heads)]
    other_plan = hand_on(plan)
    other_queries = [
        hand_on(queries[:, :, head * group * HEAD_SIZE : (head + 1) * group * HEAD_SIZE])
        for head in range(kept, kv_heads)
    ]
    gathered += [gather_turns(message) for message in swapped]
    parts = []
    for head in range(kept, kv_heads):
        packed = pack_pages(block_order, owners, messages[head], slots, page_tokens)
        parts += exchange(packed)
    staged = stage(plan, queries, *messages[:kept])
    handed = []
    for head in range(kept):
        context = attend(plan, queries, gathered[head], staged, head * group, group, page_tokens)
        handed.append(hand_on(context))
    for index, head in enumerate(range(kept, kv_heads)):
        handed.append(
            attend(other_plan, other_queries[index], gathered[head], staged, 0, group, page_tokens)
        )
    columns = [(head, turn) for head in range(kept) for turn in range(count)]
    columns += [(head, 0) for head in range(kept, kv_heads)]
    blocks = [gathered[head][turn] if head < kept else messages[head] for head, turn in columns]
    cache = scatter_pages(block_order, owners, blocks, columns, width, page_tokens, slots)
    cache_keys, cache_values, context = finish(*cache, handed, parts, list(range(kept, kv_heads)))
    return (context, cache_keys, cache_values)


def solution(mesh):
    in_specs = (
        P(("groups", "section"), "seq", "kv"),
        P(("groups", "section"), "seq", "kv"),
        P(("groups", "section"), "seq", "kv"),
        P(("groups", "section"), None),
        P(("groups", "section"), None),
        P(("groups", "section"), None, None),
    )
    out_specs = (
        P(("groups", "section"), "seq", "kv"),
        P(("groups", "section"), "seq", None, "kv"),
        P(("groups", "section"), "seq", None, "kv"),
    )
    return jax.shard_map(body, mesh=mesh, in_specs=in_specs, out_specs=out_specs, check_vma=False)
```
